32 devices in a mesh: tm: 8 (over z, x), strip: 4 (over y, core).
Axes of the slice: x: 2, y: 2, z: 4, core: 2. Of those that a mesh axis runs over, the one named last changes fastest.
Arguments:
- coarse_feat: bfloat16 [32, 48, 4, 384], P('tm', 'strip'), may hold values from -6 to 6
- coarse_gain: float32 [384], replicated, may hold values from 0.5 to 2
- coarse_weight: bfloat16 [3, 3, 3, 384, 384], replicated, may hold values from -0.0625 to 0.0625
- coarse_bias: float32 [384], replicated, may hold values from -3 to 3
- up_weight: bfloat16 [3, 3, 384, 192], replicated, may hold values from -0.109375 to 0.109375
- up_bias: float32 [192], replicated, may hold values from -3 to 3
- fine_gain: float32 [192], replicated, may hold values from 0.5 to 2
- fine_weight: bfloat16 [3, 3, 3, 192, 192], replicated, may hold values from -0.078125 to 0.078125
- fine_bias: float32 [192], replicated, may hold values from -3 to 3
Outputs:
- decoded: bfloat16 [32, 96, 8, 192], P('tm', 'strip')
The draws below stay inside these ranges and needn't reach their ends.
All inputs are finite; a program needn't handle non-finite values.
Results may differ from the reference program's by a relative error of at most 0.0095.
Values may be sent and summed in bfloat16 or wider, within the bound.
A program may use at most 64 MiB of HBM per device.

```python
import math
import jax
import jax.numpy as jnp
from jax import lax

C0 = 384
C1 = 192
WW = 4
FRAMES = 32
ROWS = 48


def steps_of(key, extent, split, low, top_value):
    def one(axis_at, parts):
        draws = jax.random.uniform(jax.random.fold_in(jax.random.fold_in(key, 6), axis_at), (parts,), jnp.float32, low / len(split), top_value / len(split))
        return jnp.repeat(jnp.exp(draws), extent[axis_at] // parts).reshape((-1,) + (1,) * (len(extent) - axis_at - 1))

    level = one(*split[0])
    for cut in split[1:]:
        level = level * one(*cut)
    return level


def gaussian(own_key, extent, width, limit, cuts=(), held_as=jnp.bfloat16):
    entries = jax.random.normal(own_key, extent, jnp.float32) * width
    if len(cuts) > 0:
        entries = steps_of(own_key, extent, cuts, -0.22, 0.18) * entries
    return jnp.clip(entries, min=-limit, max=limit).astype(held_as)


def setup_inputs(seed: int = 0) -> dict:
    keys = jax.random.split(jax.random.key(seed), 10)
    coarse_feat = gaussian(keys[0], (FRAMES, ROWS, WW, C0), 1.0, 6.0, ((0, 8), (1, 4)))
    coarse_gain = jnp.clip(jnp.exp(jax.random.uniform(keys[1], (C0,), jnp.float32, math.log(0.5), math.log(2.0))), 0.5, 2.0)
    coarse_weight = gaussian(keys[2], (3, 3, 3, C0, C0), (27 * C0) ** -0.5, 0.0625)
    coarse_bias = gaussian(keys[3], (C0,), 0.5, 3.0, (), jnp.float32)
    up_weight = gaussian(keys[4], (3, 3, C0, C1), (9 * C0) ** -0.5, 0.109375)
    up_bias = gaussian(keys[5], (C1,), 0.5, 3.0, (), jnp.float32)
    fine_gain = jnp.clip(jnp.exp(jax.random.uniform(keys[6], (C1,), jnp.float32, math.log(0.5), math.log(2.0))), 0.5, 2.0)
    fine_weight = gaussian(keys[7], (3, 3, 3, C1, C1), (27 * C1) ** -0.5, 0.078125)
    fine_bias = gaussian(keys[8], (C1,), 0.5, 3.0, (), jnp.float32)
    return dict(coarse_feat=coarse_feat, coarse_gain=coarse_gain, coarse_weight=coarse_weight, coarse_bias=coarse_bias, up_weight=up_weight, up_bias=up_bias, fine_gain=fine_gain, fine_weight=fine_weight, fine_bias=fine_bias)


eps = 1e-06

def prep(feat, gain):
    values = feat.astype(jnp.float32)
    meansq = lax.optimization_barrier(jnp.mean(values * values, axis=-1, keepdims=True))
    return jax.nn.silu(values * lax.rsqrt(meansq + eps) * gain).astype(jnp.bfloat16)

def causal_conv(act, kernel):
    out = lax.conv_general_dilated(act.astype(jnp.float32)[None], kernel.astype(jnp.float32), (1, 1, 1), [(2, 0), (1, 1), (1, 1)], dimension_numbers=('NDHWC', 'DHWIO', 'NDHWC'))
    return out[0]

def plane_conv(act, kernel):
    return lax.conv_general_dilated(act.astype(jnp.float32), kernel.astype(jnp.float32), (1, 1), [(1, 1), (1, 1)], dimension_numbers=('NHWC', 'HWIO', 'NHWC'))

def reference(coarse_feat, coarse_gain, coarse_weight, coarse_bias, up_weight, up_bias, fine_gain, fine_weight, fine_bias):
    act0 = prep(coarse_feat, coarse_gain)
    coarse = (causal_conv(act0, coarse_weight) + coarse_bias).astype(jnp.bfloat16)
    upper = jnp.repeat(jnp.repeat(coarse, 2, axis=1), 2, axis=2)
    lifted = (plane_conv(upper, up_weight) + up_bias).astype(jnp.bfloat16)
    act1 = prep(lifted, fine_gain)
    decoded = causal_conv(act1, fine_weight) + fine_bias + lifted.astype(jnp.float32)
    return decoded.astype(jnp.bfloat16)
```

```python
import functools

import jax
import jax.numpy as jnp
from jax import lax
from jax.experimental import pallas as pl
from jax.experimental.pallas import tpu as pltpu
from jax.sharding import PartitionSpec as P

eps = 1e-06
F32, BF = jnp.float32, jnp.bfloat16


def prep(values, gain):
    meansq = jnp.mean(values * values, axis=-1, keepdims=True)
    v = values * lax.rsqrt(meansq + eps) * gain
    return (v / (1.0 + jnp.exp(-v))).astype(BF)


def body(dims, x_ref, g0_ref, wc_hbm, b0_ref, wu_hbm, bu_ref, g1_ref, wf_hbm, b1_ref, out_ref,
         wc, wu, wf, acts, acc, prod, fine, resid, facc, sems):
    frames, rows, cols, pad_rows, strips = dims
    c0, c1 = wc.shape[-1], wu.shape[-1]
    tm, place = lax.axis_index("tm"), lax.axis_index("strip")
    moves = [pltpu.make_async_copy(wc_hbm.at[t], wc.at[t], sems.at[t]) for t in range(3)]
    moves.append(pltpu.make_async_copy(wu_hbm, wu, sems.at[3]))
    moves.append(pltpu.make_async_copy(wf_hbm, wf.at[:, pl.ds(0, c1), :], sems.at[4]))
    for move in moves:
        move.start()
    fl, fc = frames + 2, 2 * cols

    gain0 = g0_ref[...]
    blank = jnp.zeros((3, frames + 4, 1, pad_rows, c0), BF)
    acts[:, :, 0:1] = blank
    acts[:, :, cols + 1 :] = blank

    def first(f, _):
        a = prep(x_ref[f].astype(F32).reshape(cols * pad_rows, c0), gain0).astype(F32)
        for k, shift in enumerate((1, 0, cols * pad_rows - 1)):
            moved = pltpu.roll(a, shift, 0) if shift else a
            acts[k, f, pl.ds(1, cols)] = moved.reshape(cols, pad_rows, c0).astype(BF)
        return 0

    lax.fori_loop(0, frames + 4, first, 0)
    wf[:, pl.ds(c1, wf.shape[1] - c1), :] = jnp.zeros((27, wf.shape[1] - c1, c1), BF)
    fblank = jnp.zeros((4, fl, 1, pad_rows, fine.shape[-1]), BF)
    fine[:, :, 0:1] = fblank
    fine[:, :, fc + 1 :] = fblank
    if fine.shape[-1] > c1:
        fine[:, :, :, :, pl.ds(c1, fine.shape[-1] - c1)] = jnp.zeros(
            (4, fl, fc + 2, pad_rows, fine.shape[-1] - c1), BF)

    m = fl * cols * pad_rows
    for t in range(3):
        moves[t].wait()
        for k in range(3):
            lhs = jnp.concatenate(
                [acts[k, t : t + fl, c : c + cols].reshape(m, c0) for c in range(3)], axis=1)
            part = jnp.dot(lhs, wc[t, k].reshape(3 * c0, c0), preferred_element_type=F32)
            if t == 0 and k == 0:
                acc[...] = part + b0_ref[...]
            else:
                acc[...] += part
    row = lax.broadcasted_iota(jnp.int32, (m, 1), 0) % pad_rows + (place * rows - 2)
    keep = (row >= 0) & (row < strips * rows)
    coarse = jnp.where(keep, acc[...], 0.0).astype(BF)

    moves[3].wait()
    for r in range(3):
        for c in range(3):
            prod[r, c] = jnp.dot(coarse, wu[r, c], preferred_element_type=F32).reshape(
                fl, cols, pad_rows, c1)

    frow = 2 * (lax.broadcasted_iota(jnp.int32, (pad_rows, 1), 0) + (place * rows - 2))
    limit = 2 * strips * rows
    bias_u, gain1 = bu_ref[...], g1_ref[...]

    def lift(f, _):
        live = tm * frames + f >= 2
        for col in range(fc):
            j, b = col // 2, col % 2
            q = []
            for r in range(3):
                if b == 0:
                    s = prod[r, 1, f, j] + prod[r, 2, f, j]
                    if j > 0:
                        s = s + prod[r, 0, f, j - 1]
                else:
                    s = prod[r, 0, f, j] + prod[r, 1, f, j]
                    if j < cols - 1:
                        s = s + prod[r, 2, f, j + 1]
                q.append(s)
            pair = (pltpu.roll(q[0], 1, 0) + q[1] + q[2],
                    q[0] + q[1] + pltpu.roll(q[2], pad_rows - 1, 0))
            for a in range(2):
                at = frow + a
                ok = (at >= 0) & (at < limit) & live
                lifted = jnp.where(ok, pair[a] + bias_u, 0.0).astype(BF)
                resid[a, f, col] = lifted
                act = prep(lifted.astype(F32), gain1)
                fine[a, f, col + 1, :, pl.ds(0, c1)] = act
                moved = pltpu.roll(act.astype(F32), pad_rows - 1 if a == 0 else 1, 0)
                fine[3 - a, f, col + 1, :, pl.ds(0, c1)] = moved.astype(BF)
        return 0

    lax.fori_loop(0, fl, lift, 0)

    moves[4].wait()
    kf = fine.shape[-1]
    mf = frames * fc * pad_rows
    for a in range(2):
        planes = (2, 0, 1) if a == 0 else (0, 1, 3)
        for t in range(3):
            for k in range(3):
                lhs = jnp.concatenate(
                    [fine[planes[k], t : t + frames, c : c + fc].reshape(mf, kf) for c in range(3)],
                    axis=1)
                at = (t * 3 + k) * 3
                part = jnp.dot(lhs, wf[at : at + 3].reshape(3 * kf, c1), preferred_element_type=F32)
                if t == 0 and k == 0:
                    facc[...] = part + b1_ref[...]
                else:
                    facc[...] += part
        for f in range(frames):
            size = fc * pad_rows
            total = facc[f * size : (f + 1) * size].reshape(fc, pad_rows, c1)
            total = total + resid[a, f + 2].astype(F32)
            total = jnp.swapaxes(total, 0, 1)[2 : 2 + rows]
            out_ref[f, :, a] = total.astype(BF)


def compute(x, g0, wc, b0, wu, bu, g1, wf, b1, frames, rows, strips):
    cols, pad_rows, c0 = x.shape[1:]
    c1 = wu.shape[-1]
    kf = -(-c1 // 128) * 128
    fl, fc = frames + 2, 2 * cols
    vm = pl.BlockSpec(memory_space=pltpu.VMEM)
    hb = pl.BlockSpec(memory_space=pl.ANY)
    return pl.pallas_call(
        functools.partial(body, (frames, rows, cols, pad_rows, strips)),
        out_shape=jax.ShapeDtypeStruct((frames, rows, 2, fc, c1), BF),
        in_specs=[vm, vm, hb, vm, hb, vm, vm, hb, vm],
        out_specs=vm,
        scratch_shapes=[
            pltpu.VMEM((3, 3, 3, c0, c0), BF),
            pltpu.VMEM((3, 3, c0, c1), BF),
            pltpu.VMEM((27, kf, c1), BF),
            pltpu.VMEM((3, frames + 4, cols + 2, pad_rows, c0), BF),
            pltpu.VMEM((fl * cols * pad_rows, c0), F32),
            pltpu.VMEM((3, 3, fl, cols, pad_rows, c1), F32),
            pltpu.VMEM((4, fl, fc + 2, pad_rows, kf), BF),
            pltpu.VMEM((2, fl, fc, pad_rows, c1), BF),
            pltpu.VMEM((frames * fc * pad_rows, c1), F32),
            pltpu.SemaphoreType.DMA((5,)),
        ],
        compiler_params=pltpu.CompilerParams(vmem_limit_bytes=56 << 20),
    )(x, g0.reshape(1, c0), wc, b0.reshape(1, c0), wu, bu.reshape(1, c1), g1.reshape(1, c1),
      wf.reshape(27, c1, c1), b1.reshape(1, c1))


def local(feat, g0, wc, b0, wu, bu, g1, wf, b1):
    frames, rows, cols, c0 = feat.shape
    c1 = wu.shape[-1]
    tms, strips = lax.axis_size("tm"), lax.axis_size("strip")
    flat = [(i, j) for i in range(tms) for j in range(strips)]

    def send(value, dt, ds):
        pairs = [(i * strips + j, (i + dt) * strips + j + ds) for i, j in flat
                 if 0 <= i + dt < tms and 0 <= j + ds < strips]
        return lax.ppermute(value, ("tm", "strip"), pairs)

    high, low, late = feat[:, :2], feat[:, rows - 2 :], feat[frames - 4 :]
    now = jnp.concatenate([send(low, 0, 1), feat, send(high, 0, -1)], axis=1)
    past = jnp.concatenate([send(low[frames - 4 :], 1, 1), send(late, 1, 0),
                            send(high[frames - 4 :], 1, -1)], axis=1)
    x = jnp.concatenate([past, now], axis=0)
    pad_rows = -(-(rows + 4) // 16) * 16
    x = jnp.pad(x, ((0, 0), (0, pad_rows - rows - 4), (0, 0), (0, 0)))
    x = x.transpose(0, 2, 1, 3)
    out = compute(x, g0, wc, b0, wu, bu, g1, wf, b1, frames, rows, strips)
    return out.reshape(frames, 2 * rows, 2 * cols, c1)


def solution(mesh):
    placed = (P("tm", "strip", None, None), P(), P(), P(), P(), P(), P(), P(), P())
    return jax.shard_map(
        local, mesh=mesh, in_specs=placed, out_specs=P("tm", "strip", None, None), check_vma=False
    )
```

```python
import functools

import jax
import jax.numpy as jnp
from jax import lax
from jax.experimental import pallas as pl
from jax.experimental.pallas import tpu as pltpu
from jax.sharding import PartitionSpec as P

eps = 1e-06
F32, BF = jnp.float32, jnp.bfloat16


def prep(values, gain):
    meansq = jnp.mean(values * values, axis=-1, keepdims=True)
    v = values * lax.rsqrt(meansq + eps) * gain
    return (v / (1.0 + jnp.exp(-v))).astype(BF)


def halo(dims, feat, ext, send_sems, recv_sems):
    frames, rows, tms, strips = dims
    tm, place = lax.axis_index("tm"), lax.axis_index("strip")

    def inside(dt, ds):
        return (tm + dt >= 0) & (tm + dt < tms) & (place + ds >= 0) & (place + ds < strips)

    own, late, top, low = (pl.ds(n, k) for n, k in ((4, frames), (frames - 4, 4), (0, 2), (rows - 2, 2)))
    past, every, above, below = pl.ds(0, 4), pl.ds(0, frames), pl.ds(0, 2), pl.ds(rows + 2, 2)
    plan = ((1, 0, (late, pl.ds(0, rows)), (past, pl.ds(2, rows))),
            (0, 1, (every, low), (own, above)),
            (0, -1, (every, top), (own, below)),
            (1, 1, (late, low), (past, above)),
            (1, -1, (late, top), (past, below)))
    barrier = pltpu.get_barrier_semaphore()
    expected = 0
    for dt, ds, _, _ in plan:
        @pl.when(inside(-dt, -ds))
        def _(dt=dt, ds=ds):
            pl.semaphore_signal(barrier, inc=1, device_id=(tm - dt, place - ds),
                                device_id_type=pl.DeviceIdType.MESH)
        expected = expected + inside(dt, ds).astype(jnp.int32)
    pl.semaphore_wait(barrier, expected)

    def move(n):
        dt, ds, src, dst = plan[n]
        return pltpu.make_async_remote_copy(
            src_ref=feat.at[src], dst_ref=ext.at[dst], send_sem=send_sems.at[n],
            recv_sem=recv_sems.at[n], device_id=(tm + dt, place + ds),
            device_id_type=pl.DeviceIdType.MESH)

    for n, (dt, ds, _, _) in enumerate(plan):
        @pl.when(inside(dt, ds))
        def _(n=n):
            move(n).start()

    def finish():
        for n, (dt, ds, _, dst) in enumerate(plan):
            @pl.when(inside(-dt, -ds))
            def _(n=n):
                move(n).wait_recv()

            @pl.when(inside(dt, ds))
            def _(n=n):
                move(n).wait_send()

    def fill():
        ext[own, pl.ds(2, rows)] = feat[...]
        for dt, ds, _, dst in plan:
            @pl.when(jnp.logical_not(inside(-dt, -ds)))
            def _(dst=dst):
                ext[dst] = jnp.zeros((dst[0].size, dst[1].size) + ext.shape[2:], BF)
        spare = ext.shape[1] - rows - 4
        if spare:
            ext[:, pl.ds(rows + 4, spare)] = jnp.zeros((ext.shape[0], spare) + ext.shape[2:], BF)

    return fill, finish


def body(dims, feat_ref, g0_ref, wc_hbm, b0_ref, wu_hbm, bu_ref, g1_ref, wf_hbm, b1_ref, out_ref,
         ext, wc, wu, wf, acts, acc, prod, fine, resid, facc, sems, send_sems, recv_sems):
    frames, rows, cols, pad_rows, tms, strips = dims
    c0, c1 = wc.shape[-1], wf.shape[-1]
    tm, place = lax.axis_index("tm"), lax.axis_index("strip")
    fill, finish = halo((frames, rows, tms, strips), feat_ref, ext, send_sems, recv_sems)
    moves = [pltpu.make_async_copy(wc_hbm.at[t], wc.at[t], sems.at[t]) for t in range(3)]
    moves.append(pltpu.make_async_copy(wu_hbm, wu, sems.at[3]))
    moves.append(pltpu.make_async_copy(wf_hbm, wf.at[:, pl.ds(0, c1), :], sems.at[4]))
    for move in moves:
        move.start()
    fill()
    fl, fc = frames + 2, 2 * cols

    gain0 = g0_ref[...].reshape(1, c0)
    blank = jnp.zeros((3, frames + 4, 1, pad_rows, c0), BF)
    acts[:, :, 0:1] = blank
    acts[:, :, cols + 1 :] = blank

    wf[:, pl.ds(c1, wf.shape[1] - c1), :] = jnp.zeros((27, wf.shape[1] - c1, c1), BF)
    fblank = jnp.zeros((4, fl, 1, pad_rows, fine.shape[-1]), BF)
    fine[:, :, 0:1] = fblank
    fine[:, :, fc + 1 :] = fblank
    if fine.shape[-1] > c1:
        fine[:, :, :, :, pl.ds(c1, fine.shape[-1] - c1)] = jnp.zeros(
            (4, fl, fc + 2, pad_rows, fine.shape[-1] - c1), BF)

    finish()

    def first(f, _):
        x = jnp.swapaxes(ext[f].astype(F32), 0, 1).reshape(cols * pad_rows, c0)
        a = prep(x, gain0).astype(F32)
        for k, shift in enumerate((1, 0, cols * pad_rows - 1)):
            moved = pltpu.roll(a, shift, 0) if shift else a
            acts[k, f, pl.ds(1, cols)] = moved.reshape(cols, pad_rows, c0).astype(BF)
        return 0

    lax.fori_loop(0, frames + 4, first, 0)
    m = fl * cols * pad_rows
    for t in range(3):
        moves[t].wait()
        for k in range(3):
            lhs = jnp.concatenate(
                [acts[k, t : t + fl, c : c + cols].reshape(m, c0) for c in range(3)], axis=1)
            part = jnp.dot(lhs, wc[t, k].reshape(3 * c0, c0), preferred_element_type=F32)
            if t == 0 and k == 0:
                acc[...] = part + b0_ref[...].reshape(1, c0)
            else:
                acc[...] += part
    row = lax.broadcasted_iota(jnp.int32, (m, 1), 0) % pad_rows + (place * rows - 2)
    keep = (row >= 0) & (row < strips * rows)
    coarse = jnp.where(keep, acc[...], 0.0).astype(BF)

    moves[3].wait()
    for r in range(3):
        for c in range(3):
            prod[r, c] = lax.dot_general(
                coarse, wu[r, c], (((1,), (1,)), ((), ())), preferred_element_type=F32).reshape(
                fl, cols, pad_rows, c1)

    frow = 2 * (lax.broadcasted_iota(jnp.int32, (pad_rows, 1), 0) + (place * rows - 2))
    limit = 2 * strips * rows
    bias_u, gain1 = bu_ref[...].reshape(1, c1), g1_ref[...].reshape(1, c1)

    def lift(f, _):
        live = tm * frames + f >= 2
        for col in range(fc):
            j, b = col // 2, col % 2
            q = []
            for r in range(3):
                if b == 0:
                    s = prod[r, 1, f, j] + prod[r, 2, f, j]
                    if j > 0:
                        s = s + prod[r, 0, f, j - 1]
                else:
                    s = prod[r, 0, f, j] + prod[r, 1, f, j]
                    if j < cols - 1:
                        s = s + prod[r, 2, f, j + 1]
                q.append(s)
            pair = (pltpu.roll(q[0], 1, 0) + q[1] + q[2],
                    q[0] + q[1] + pltpu.roll(q[2], pad_rows - 1, 0))
            for a in range(2):
                at = frow + a
                ok = (at >= 0) & (at < limit) & live
                lifted = jnp.where(ok, pair[a] + bias_u, 0.0).astype(BF)
                resid[a, f, col] = lifted
                act = prep(lifted.astype(F32), gain1)
                fine[a, f, col + 1, :, pl.ds(0, c1)] = act
                moved = pltpu.roll(act.astype(F32), pad_rows - 1 if a == 0 else 1, 0)
                fine[3 - a, f, col + 1, :, pl.ds(0, c1)] = moved.astype(BF)
        return 0

    lax.fori_loop(0, fl, lift, 0)

    moves[4].wait()
    kf = fine.shape[-1]
    mf = frames * fc * pad_rows
    for a in range(2):
        planes = (2, 0, 1) if a == 0 else (0, 1, 3)
        for t in range(3):
            for k in range(3):
                lhs = jnp.concatenate(
                    [fine[planes[k], t : t + frames, c : c + fc].reshape(mf, kf) for c in range(3)],
                    axis=1)
                at = (t * 3 + k) * 3
                part = jnp.dot(lhs, wf[at : at + 3].reshape(3 * kf, c1), preferred_element_type=F32)
                if t == 0 and k == 0:
                    facc[...] = part + b1_ref[...].reshape(1, c1)
                else:
                    facc[...] += part
        for f in range(frames):
            size = fc * pad_rows
            total = facc[f * size : (f + 1) * size].reshape(fc, pad_rows, c1)
            total = total + resid[a, f + 2].astype(F32)
            total = jnp.swapaxes(total, 0, 1)[2 : 2 + rows]
            out_ref[f, :, a] = total.astype(BF)


def local(feat, g0, wc, b0, wu, bu, g1, wf, b1):
    frames, rows, cols, c0 = feat.shape
    c1 = wu.shape[-1]
    tms, strips = lax.axis_size("tm"), lax.axis_size("strip")
    pad_rows = -(-(rows + 4) // 16) * 16
    kf = -(-c1 // 128) * 128
    fl, fc = frames + 2, 2 * cols
    vm = pl.BlockSpec(memory_space=pltpu.VMEM)
    hb = pl.BlockSpec(memory_space=pl.ANY)
    out = pl.pallas_call(
        functools.partial(body, (frames, rows, cols, pad_rows, tms, strips)),
        out_shape=jax.ShapeDtypeStruct((frames, rows, 2, fc, c1), BF),
        in_specs=[vm, vm, hb, vm, hb, vm, vm, hb, vm],
        out_specs=vm,
        scratch_shapes=[
            pltpu.VMEM((frames + 4, pad_rows, cols, c0), BF),
            pltpu.VMEM((3, 3, 3, c0, c0), BF),
            pltpu.VMEM((3, 3, c1, c0), BF),
            pltpu.VMEM((27, kf, c1), BF),
            pltpu.VMEM((3, frames + 4, cols + 2, pad_rows, c0), BF),
            pltpu.VMEM((fl * cols * pad_rows, c0), F32),
            pltpu.VMEM((3, 3, fl, cols, pad_rows, c1), F32),
            pltpu.VMEM((4, fl, fc + 2, pad_rows, kf), BF),
            pltpu.VMEM((2, fl, fc, pad_rows, c1), BF),
            pltpu.VMEM((frames * fc * pad_rows, c1), F32),
            pltpu.SemaphoreType.DMA((5,)),
            pltpu.SemaphoreType.DMA((5,)),
            pltpu.SemaphoreType.DMA((5,)),
        ],
        compiler_params=pltpu.CompilerParams(
            vmem_limit_bytes=56 << 20, collective_id=0, has_side_effects=True),
    )(feat, g0, wc, b0, jnp.swapaxes(wu, 2, 3), bu, g1, wf.reshape(27, c1, c1), b1)
    return out.reshape(frames, 2 * rows, fc, c1)


def solution(mesh):
    placed = (P("tm", "strip", None, None), P(), P(), P(), P(), P(), P(), P(), P())
    return jax.shard_map(
        local, mesh=mesh, in_specs=placed, out_specs=P("tm", "strip", None, None), check_vma=False
    )
```

```python
import functools

import jax
import jax.numpy as jnp
from jax import lax
from jax.experimental import pallas as pl
from jax.experimental.pallas import tpu as pltpu
from jax.sharding import PartitionSpec as P

eps = 1e-06
F32, BF = jnp.float32, jnp.bfloat16


def prep(values, gain):
    meansq = jnp.mean(values * values, axis=-1, keepdims=True)
    v = values * lax.rsqrt(meansq + eps) * gain
    return (v / (1.0 + jnp.exp(-v))).astype(BF)


def halo(dims, feat, ext, send_sems, recv_sems):
    frames, rows, tms, strips = dims
    tm, place = lax.axis_index("tm"), lax.axis_index("strip")

    def inside(dt, ds):
        return (tm + dt >= 0) & (tm + dt < tms) & (place + ds >= 0) & (place + ds < strips)

    own, late, top, low = (pl.ds(n, k) for n, k in ((4, frames), (frames - 4, 4), (0, 2), (rows - 2, 2)))
    past, every, above, below = pl.ds(0, 4), pl.ds(0, frames), pl.ds(0, 2), pl.ds(rows + 2, 2)
    plan = ((0, 1, (every, low), (own, above)),
            (0, -1, (every, top), (own, below)),
            (1, 1, (late, low), (past, above)),
            (1, -1, (late, top), (past, below)),
            (1, 0, (late, pl.ds(0, rows)), (past, pl.ds(2, rows))))
    barrier = pltpu.get_barrier_semaphore()
    expected = 0
    for dt, ds, _, _ in plan:
        @pl.when(inside(-dt, -ds))
        def _(dt=dt, ds=ds):
            pl.semaphore_signal(barrier, inc=1, device_id=(tm - dt, place - ds),
                                device_id_type=pl.DeviceIdType.MESH)
        expected = expected + inside(dt, ds).astype(jnp.int32)
    pl.semaphore_wait(barrier, expected)

    def move(n):
        dt, ds, src, dst = plan[n]
        return pltpu.make_async_remote_copy(
            src_ref=feat.at[src], dst_ref=ext.at[dst], send_sem=send_sems.at[n],
            recv_sem=recv_sems.at[n], device_id=(tm + dt, place + ds),
            device_id_type=pl.DeviceIdType.MESH)

    for n, (dt, ds, _, _) in enumerate(plan):
        @pl.when(inside(dt, ds))
        def _(n=n):
            move(n).start()

    def arrive(first, last):
        for n in range(first, last):
            @pl.when(inside(-plan[n][0], -plan[n][1]))
            def _(n=n):
                move(n).wait_recv()

    def depart():
        for n, (dt, ds, _, _) in enumerate(plan):
            @pl.when(inside(dt, ds))
            def _(n=n):
                move(n).wait_send()

    def fill():
        ext[own, pl.ds(2, rows)] = feat[...]
        for dt, ds, _, dst in plan:
            @pl.when(jnp.logical_not(inside(-dt, -ds)))
            def _(dst=dst):
                ext[dst] = jnp.zeros((dst[0].size, dst[1].size) + ext.shape[2:], BF)
        spare = ext.shape[1] - rows - 4
        if spare:
            ext[:, pl.ds(rows + 4, spare)] = jnp.zeros((ext.shape[0], spare) + ext.shape[2:], BF)

    return fill, arrive, depart


def body(dims, feat_ref, g0_ref, wc_hbm, b0_ref, wu_hbm, bu_ref, g1_ref, wf_hbm, b1_ref, out_ref,
         ext, wc, wu, wf, acts, acc, prod, fine, resid, facc, sems, send_sems, recv_sems):
    frames, rows, cols, pad_rows, tms, strips = dims
    c0, c1 = wc.shape[-1], wf.shape[-1]
    tm, place = lax.axis_index("tm"), lax.axis_index("strip")
    fill, arrive, depart = halo((frames, rows, tms, strips), feat_ref, ext, send_sems, recv_sems)
    moves = [pltpu.make_async_copy(wc_hbm.at[t], wc.at[t], sems.at[t]) for t in range(3)]
    moves.append(pltpu.make_async_copy(wu_hbm, wu, sems.at[3]))
    moves.append(pltpu.make_async_copy(wf_hbm, wf.at[:, pl.ds(0, c1), :], sems.at[4]))
    for move in moves:
        move.start()
    fill()
    fl, fc = frames + 2, 2 * cols

    gain0 = g0_ref[...].reshape(1, c0)
    blank = jnp.zeros((3, frames + 4, 1, pad_rows, c0), BF)
    acts[:, :, 0:1] = blank
    acts[:, :, cols + 1 :] = blank

    wf[:, pl.ds(c1, wf.shape[1] - c1), :] = jnp.zeros((27, wf.shape[1] - c1, c1), BF)
    fblank = jnp.zeros((4, fl, 1, pad_rows, fine.shape[-1]), BF)
    fine[:, :, 0:1] = fblank
    fine[:, :, fc + 1 :] = fblank
    if fine.shape[-1] > c1:
        fine[:, :, :, :, pl.ds(c1, fine.shape[-1] - c1)] = jnp.zeros(
            (4, fl, fc + 2, pad_rows, fine.shape[-1] - c1), BF)

    def first(f, _):
        x = jnp.swapaxes(ext[f].astype(F32), 0, 1).reshape(cols * pad_rows, c0)
        a = prep(x, gain0).astype(F32)
        for k, shift in enumerate((1, 0, cols * pad_rows - 1)):
            moved = pltpu.roll(a, shift, 0) if shift else a
            acts[k, f, pl.ds(1, cols)] = moved.reshape(cols, pad_rows, c0).astype(BF)
        return 0

    def convolve(lo, hi, fresh):
        n = hi - lo
        m = n * cols * pad_rows
        for t in range(3):
            if fresh:
                moves[t].wait()
            for k in range(3):
                lhs = jnp.concatenate(
                    [acts[k, lo + t : hi + t, c : c + cols].reshape(m, c0) for c in range(3)],
                    axis=1)
                part = jnp.dot(lhs, wc[t, k].reshape(3 * c0, c0), preferred_element_type=F32)
                if t == 0 and k == 0:
                    acc[:m] = part + b0_ref[...].reshape(1, c0)
                else:
                    acc[:m] += part
        row = lax.broadcasted_iota(jnp.int32, (m, 1), 0) % pad_rows + (place * rows - 2)
        keep = (row >= 0) & (row < strips * rows)
        coarse = jnp.where(keep, acc[:m], 0.0).astype(BF)
        if fresh:
            moves[3].wait()
        for r in range(3):
            for c in range(3):
                prod[r, c, lo:hi] = lax.dot_general(
                    coarse, wu[r, c], (((1,), (1,)), ((), ())), preferred_element_type=F32
                ).reshape(n, cols, pad_rows, c1)

    frow = 2 * (lax.broadcasted_iota(jnp.int32, (pad_rows, 1), 0) + (place * rows - 2))
    limit = 2 * strips * rows
    bias_u, gain1 = bu_ref[...].reshape(1, c1), g1_ref[...].reshape(1, c1)

    def lift(f, _):
        live = tm * frames + f >= 2
        for col in range(fc):
            j, b = col // 2, col % 2
            q = []
            for r in range(3):
                if b == 0:
                    s = prod[r, 1, f, j] + prod[r, 2, f, j]
                    if j > 0:
                        s = s + prod[r, 0, f, j - 1]
                else:
                    s = prod[r, 0, f, j] + prod[r, 1, f, j]
                    if j < cols - 1:
                        s = s + prod[r, 2, f, j + 1]
                q.append(s)
            pair = (pltpu.roll(q[0], 1, 0) + q[1] + q[2],
                    q[0] + q[1] + pltpu.roll(q[2], pad_rows - 1, 0))
            for a in range(2):
                at = frow + a
                ok = (at >= 0) & (at < limit) & live
                lifted = jnp.where(ok, pair[a] + bias_u, 0.0).astype(BF)
                resid[a, f, col] = lifted
                act = prep(lifted.astype(F32), gain1)
                fine[a, f, col + 1, :, pl.ds(0, c1)] = act
                moved = pltpu.roll(act.astype(F32), pad_rows - 1 if a == 0 else 1, 0)
                fine[3 - a, f, col + 1, :, pl.ds(0, c1)] = moved.astype(BF)
        return 0

    arrive(0, 2)
    lax.fori_loop(4, frames + 4, first, 0)
    convolve(4, fl, True)
    lax.fori_loop(4, fl, lift, 0)
    arrive(2, 5)
    lax.fori_loop(0, 4, first, 0)
    convolve(0, 4, False)
    lax.fori_loop(0, 4, lift, 0)

    moves[4].wait()
    kf = fine.shape[-1]
    mf = frames * fc * pad_rows
    for a in range(2):
        planes = (2, 0, 1) if a == 0 else (0, 1, 3)
        for t in range(3):
            for k in range(3):
                lhs = jnp.concatenate(
                    [fine[planes[k], t : t + frames, c : c + fc].reshape(mf, kf) for c in range(3)],
                    axis=1)
                at = (t * 3 + k) * 3
                part = jnp.dot(lhs, wf[at : at + 3].reshape(3 * kf, c1), preferred_element_type=F32)
                if t == 0 and k == 0:
                    facc[...] = part + b1_ref[...].reshape(1, c1)
                else:
                    facc[...] += part
        for f in range(frames):
            size = fc * pad_rows
            total = facc[f * size : (f + 1) * size].reshape(fc, pad_rows, c1)
            total = total + resid[a, f + 2].astype(F32)
            total = jnp.swapaxes(total, 0, 1)[2 : 2 + rows]
            out_ref[f, :, a] = total.astype(BF)
    depart()


def local(feat, g0, wc, b0, wu, bu, g1, wf, b1):
    frames, rows, cols, c0 = feat.shape
    c1 = wu.shape[-1]
    tms, strips = lax.axis_size("tm"), lax.axis_size("strip")
    pad_rows = -(-(rows + 4) // 16) * 16
    kf = -(-c1 // 128) * 128
    fl, fc = frames + 2, 2 * cols
    vm = pl.BlockSpec(memory_space=pltpu.VMEM)
    hb = pl.BlockSpec(memory_space=pl.ANY)
    out = pl.pallas_call(
        functools.partial(body, (frames, rows, cols, pad_rows, tms, strips)),
        out_shape=jax.ShapeDtypeStruct((frames, rows, 2, fc, c1), BF),
        in_specs=[vm, vm, hb, vm, hb, vm, vm, hb, vm],
        out_specs=vm,
        scratch_shapes=[
            pltpu.VMEM((frames + 4, pad_rows, cols, c0), BF),
            pltpu.VMEM((3, 3, 3, c0, c0), BF),
            pltpu.VMEM((3, 3, c1, c0), BF),
            pltpu.VMEM((27, kf, c1), BF),
            pltpu.VMEM((3, frames + 4, cols + 2, pad_rows, c0), BF),
            pltpu.VMEM((fl * cols * pad_rows, c0), F32),
            pltpu.VMEM((3, 3, fl, cols, pad_rows, c1), F32),
            pltpu.VMEM((4, fl, fc + 2, pad_rows, kf), BF),
            pltpu.VMEM((2, fl, fc, pad_rows, c1), BF),
            pltpu.VMEM((frames * fc * pad_rows, c1), F32),
            pltpu.SemaphoreType.DMA((5,)),
            pltpu.SemaphoreType.DMA((5,)),
            pltpu.SemaphoreType.DMA((5,)),
        ],
        compiler_params=pltpu.CompilerParams(
            vmem_limit_bytes=56 << 20, collective_id=0, has_side_effects=True),
    )(feat, g0, wc, b0, jnp.swapaxes(wu, 2, 3), bu, g1, wf.reshape(27, c1, c1), b1)
    return out.reshape(frames, 2 * rows, fc, c1)


def solution(mesh):
    placed = (P("tm", "strip", None, None), P(), P(), P(), P(), P(), P(), P(), P())
    return jax.shard_map(
        local, mesh=mesh, in_specs=placed, out_specs=P("tm", "strip", None, None), check_vma=False
    )
```

```python
import functools

import jax
import jax.numpy as jnp
from jax import lax
from jax.experimental import pallas as pl
from jax.experimental.pallas import tpu as pltpu
from jax.sharding import PartitionSpec as P

eps = 1e-06
F32, BF = jnp.float32, jnp.bfloat16


def prep(values, gain):
    meansq = jnp.mean(values * values, axis=-1, keepdims=True)
    v = values * lax.rsqrt(meansq + eps) * gain
    return (v / (1.0 + jnp.exp(-v))).astype(BF)


def halo(dims, feat, ext, send_sems, recv_sems):
    frames, rows, tms, strips = dims
    tm, place = lax.axis_index("tm"), lax.axis_index("strip")

    def inside(dt, ds):
        return (tm + dt >= 0) & (tm + dt < tms) & (place + ds >= 0) & (place + ds < strips)

    own, late, top, low = (pl.ds(n, k) for n, k in ((4, frames), (frames - 4, 4), (0, 2), (rows - 2, 2)))
    past, every, above, below = pl.ds(0, 4), pl.ds(0, frames), pl.ds(0, 2), pl.ds(rows + 2, 2)
    plan = ((0, 1, (every, low), (own, above)),
            (0, -1, (every, top), (own, below)),
            (1, 1, (late, low), (past, above)),
            (1, -1, (late, top), (past, below)),
            (1, 0, (late, pl.ds(0, rows)), (past, pl.ds(2, rows))))
    barrier = pltpu.get_barrier_semaphore()
    expected = 0
    for dt, ds, _, _ in plan:
        @pl.when(inside(-dt, -ds))
        def _(dt=dt, ds=ds):
            pl.semaphore_signal(barrier, inc=1, device_id=(tm - dt, place - ds),
                                device_id_type=pl.DeviceIdType.MESH)
        expected = expected + inside(dt, ds).astype(jnp.int32)
    pl.semaphore_wait(barrier, expected)

    def move(n):
        dt, ds, src, dst = plan[n]
        return pltpu.make_async_remote_copy(
            src_ref=feat.at[src], dst_ref=ext.at[dst], send_sem=send_sems.at[n],
            recv_sem=recv_sems.at[n], device_id=(tm + dt, place + ds),
            device_id_type=pl.DeviceIdType.MESH)

    for n, (dt, ds, _, _) in enumerate(plan):
        @pl.when(inside(dt, ds))
        def _(n=n):
            move(n).start()

    def arrive(first, last):
        for n in range(first, last):
            @pl.when(inside(-plan[n][0], -plan[n][1]))
            def _(n=n):
                move(n).wait_recv()

    def depart():
        for n, (dt, ds, _, _) in enumerate(plan):
            @pl.when(inside(dt, ds))
            def _(n=n):
                move(n).wait_send()

    def fill():
        for dt, ds, _, dst in plan:
            @pl.when(jnp.logical_not(inside(-dt, -ds)))
            def _(dst=dst):
                ext[dst] = jnp.zeros((dst[0].size, dst[1].size) + ext.shape[2:], BF)
        spare = ext.shape[1] - rows - 4
        if spare:
            ext[:, pl.ds(rows + 4, spare)] = jnp.zeros((ext.shape[0], spare) + ext.shape[2:], BF)

    return fill, arrive, depart


def body(dims, feat_ref, g0_hbm, wc_hbm, b0_hbm, wu_hbm, bu_hbm, g1_hbm, wf_hbm, b1_hbm, out_ref,
         ext, g0_ref, b0_ref, bu_ref, g1_ref, b1_ref, wc, wu, wf, acts, acc, prod, fine, resid, facc, sems, send_sems, recv_sems):
    frames, rows, cols, pad_rows, tms, strips = dims
    c0, c1 = wc.shape[-1], wf.shape[-1]
    tm, place = lax.axis_index("tm"), lax.axis_index("strip")
    fill, arrive, depart = halo((frames, rows, tms, strips), feat_ref, ext, send_sems, recv_sems)
    own = ext.at[pl.ds(4, frames), pl.ds(2, rows)]
    small = [pltpu.make_async_copy(src, dst, sems.at[5 + n]) for n, (src, dst) in enumerate((
        (feat_ref, own), (g0_hbm, g0_ref), (b0_hbm, b0_ref), (bu_hbm, bu_ref), (g1_hbm, g1_ref),
        (b1_hbm, b1_ref)))]
    moves = [pltpu.make_async_copy(wc_hbm.at[t], wc.at[t], sems.at[t]) for t in range(3)]
    moves.append(pltpu.make_async_copy(wu_hbm, wu, sems.at[3]))
    moves.append(pltpu.make_async_copy(wf_hbm, wf.at[:, pl.ds(0, c1), :], sems.at[4]))
    for move in small + moves:
        move.start()
    fill()
    fl, fc = frames + 2, 2 * cols

    blank = jnp.zeros((3, frames + 4, 1, pad_rows, c0), BF)
    acts[:, :, 0:1] = blank
    acts[:, :, cols + 1 :] = blank

    wf[:, pl.ds(c1, wf.shape[1] - c1), :] = jnp.zeros((27, wf.shape[1] - c1, c1), BF)
    fblank = jnp.zeros((4, fl, 1, pad_rows, fine.shape[-1]), BF)
    fine[:, :, 0:1] = fblank
    fine[:, :, fc + 1 :] = fblank
    if fine.shape[-1] > c1:
        fine[:, :, :, :, pl.ds(c1, fine.shape[-1] - c1)] = jnp.zeros(
            (4, fl, fc + 2, pad_rows, fine.shape[-1] - c1), BF)

    def first(f, _):
        x = jnp.swapaxes(ext[f].astype(F32), 0, 1).reshape(cols * pad_rows, c0)
        a = prep(x, g0_ref[...].reshape(1, c0)).astype(F32)
        for k, shift in enumerate((1, 0, cols * pad_rows - 1)):
            moved = pltpu.roll(a, shift, 0) if shift else a
            acts[k, f, pl.ds(1, cols)] = moved.reshape(cols, pad_rows, c0).astype(BF)
        return 0

    def convolve(lo, hi, fresh):
        n = hi - lo
        m = n * cols * pad_rows
        for t in range(3):
            if fresh:
                moves[t].wait()
            for k in range(3):
                lhs = jnp.concatenate(
                    [acts[k, lo + t : hi + t, c : c + cols].reshape(m, c0) for c in range(3)],
                    axis=1)
                part = jnp.dot(lhs, wc[t, k].reshape(3 * c0, c0), preferred_element_type=F32)
                if t == 0 and k == 0:
                    acc[:m] = part + b0_ref[...].reshape(1, c0)
                else:
                    acc[:m] += part
        row = lax.broadcasted_iota(jnp.int32, (m, 1), 0) % pad_rows + (place * rows - 2)
        keep = (row >= 0) & (row < strips * rows)
        coarse = jnp.where(keep, acc[:m], 0.0).astype(BF)
        if fresh:
            moves[3].wait()
        for r in range(3):
            for c in range(3):
                prod[r, c, lo:hi] = lax.dot_general(
                    coarse, wu[r, c], (((1,), (1,)), ((), ())), preferred_element_type=F32
                ).reshape(n, cols, pad_rows, c1)

    frow = 2 * (lax.broadcasted_iota(jnp.int32, (pad_rows, 1), 0) + (place * rows - 2))
    limit = 2 * strips * rows

    def lift(f, _):
        live = tm * frames + f >= 2
        for col in range(fc):
            j, b = col // 2, col % 2
            q = []
            for r in range(3):
                if b == 0:
                    s = prod[r, 1, f, j] + prod[r, 2, f, j]
                    if j > 0:
                        s = s + prod[r, 0, f, j - 1]
                else:
                    s = prod[r, 0, f, j] + prod[r, 1, f, j]
                    if j < cols - 1:
                        s = s + prod[r, 2, f, j + 1]
                q.append(s)
            pair = (pltpu.roll(q[0], 1, 0) + q[1] + q[2],
                    q[0] + q[1] + pltpu.roll(q[2], pad_rows - 1, 0))
            for a in range(2):
                at = frow + a
                ok = (at >= 0) & (at < limit) & live
                lifted = jnp.where(ok, pair[a] + bu_ref[...].reshape(1, c1), 0.0).astype(BF)
                resid[a, f, col] = lifted
                act = prep(lifted.astype(F32), g1_ref[...].reshape(1, c1))
                fine[a, f, col + 1, :, pl.ds(0, c1)] = act
                moved = pltpu.roll(act.astype(F32), pad_rows - 1 if a == 0 else 1, 0)
                fine[3 - a, f, col + 1, :, pl.ds(0, c1)] = moved.astype(BF)
        return 0

    for move in small:
        move.wait()
    arrive(0, 2)
    lax.fori_loop(4, frames + 4, first, 0)
    convolve(4, fl, True)
    lax.fori_loop(4, fl, lift, 0)
    arrive(2, 5)
    lax.fori_loop(0, 4, first, 0)
    convolve(0, 4, False)
    lax.fori_loop(0, 4, lift, 0)

    moves[4].wait()
    kf = fine.shape[-1]
    mf = frames * fc * pad_rows
    for a in range(2):
        planes = (2, 0, 1) if a == 0 else (0, 1, 3)
        for t in range(3):
            for k in range(3):
                lhs = jnp.concatenate(
                    [fine[planes[k], t : t + frames, c : c + fc].reshape(mf, kf) for c in range(3)],
                    axis=1)
                at = (t * 3 + k) * 3
                part = jnp.dot(lhs, wf[at : at + 3].reshape(3 * kf, c1), preferred_element_type=F32)
                if t == 0 and k == 0:
                    facc[...] = part + b1_ref[...].reshape(1, c1)
                else:
                    facc[...] += part
        for f in range(frames):
            size = fc * pad_rows
            total = facc[f * size : (f + 1) * size].reshape(fc, pad_rows, c1)
            total = total + resid[a, f + 2].astype(F32)
            total = jnp.swapaxes(total, 0, 1)[2 : 2 + rows]
            out_ref[f, :, a] = total.astype(BF)
    depart()


def local(feat, g0, wc, b0, wu, bu, g1, wf, b1):
    frames, rows, cols, c0 = feat.shape
    c1 = wu.shape[-1]
    tms, strips = lax.axis_size("tm"), lax.axis_size("strip")
    pad_rows = -(-(rows + 4) // 16) * 16
    kf = -(-c1 // 128) * 128
    fl, fc = frames + 2, 2 * cols
    vm = pl.BlockSpec(memory_space=pltpu.VMEM)
    hb = pl.BlockSpec(memory_space=pltpu.HBM)
    out = pl.pallas_call(
        functools.partial(body, (frames, rows, cols, pad_rows, tms, strips)),
        out_shape=jax.ShapeDtypeStruct((frames, rows, 2, fc, c1), BF),
        in_specs=[hb] * 9,
        out_specs=vm,
        scratch_shapes=[
            pltpu.VMEM((frames + 4, pad_rows, cols, c0), BF),
            pltpu.VMEM((c0,), F32),
            pltpu.VMEM((c0,), F32),
            pltpu.VMEM((c1,), F32),
            pltpu.VMEM((c1,), F32),
            pltpu.VMEM((c1,), F32),
            pltpu.VMEM((3, 3, 3, c0, c0), BF),
            pltpu.VMEM((3, 3, c1, c0), BF),
            pltpu.VMEM((27, kf, c1), BF),
            pltpu.VMEM((3, frames + 4, cols + 2, pad_rows, c0), BF),
            pltpu.VMEM((fl * cols * pad_rows, c0), F32),
            pltpu.VMEM((3, 3, fl, cols, pad_rows, c1), F32),
            pltpu.VMEM((4, fl, fc + 2, pad_rows, kf), BF),
            pltpu.VMEM((2, fl, fc, pad_rows, c1), BF),
            pltpu.VMEM((frames * fc * pad_rows, c1), F32),
            pltpu.SemaphoreType.DMA((11,)),
            pltpu.SemaphoreType.DMA((5,)),
            pltpu.SemaphoreType.DMA((5,)),
        ],
        compiler_params=pltpu.CompilerParams(
            vmem_limit_bytes=56 << 20, collective_id=0, has_side_effects=True),
    )(feat, g0, wc, b0, jnp.swapaxes(wu, 2, 3), bu, g1, wf.reshape(27, c1, c1), b1)
    return out.reshape(frames, 2 * rows, fc, c1)


def solution(mesh):
    placed = (P("tm", "strip", None, None), P(), P(), P(), P(), P(), P(), P(), P())
    return jax.shard_map(
        local, mesh=mesh, in_specs=placed, out_specs=P("tm", "strip", None, None), check_vma=False
    )
```
